32 devices in a mesh: grp: 4 (over x, core), seq: 8 (over z, y).
Axes of the slice: x: 2, y: 2, z: 4, core: 2. Of those that a mesh axis runs over, the one named last changes fastest.
Arguments:
- layer_input: bfloat16 [4096, 1024], P(('grp', 'seq')), may hold values from -6 to 6
- segments: int32 [4096], P(('grp', 'seq')), may hold values from 0 to 7, never falling along the last dimension, each value on 1 to 1024 neighbouring positions
- routes: int32 [4096, 8], P(('grp', 'seq')), may hold values from 0 to 31, all different within a row; in each aligned block of 128 rows (0 to 127, 128 to 255, ...) at most 34 rows name the same one
- gate_probs: float32 [4096, 8], P(('grp', 'seq')), may hold values from 0.05 to 0.3
- cotangent: bfloat16 [4096, 1024], P(('grp', 'seq')), may hold values from -6 to 6
- query_weight: bfloat16 [1024, 1024], P(('grp', 'seq')), may hold values from -0.1875 to 0.1875
- key_matrix: bfloat16 [1024, 512], P(('grp', 'seq')), may hold values from -0.1875 to 0.1875
- value_matrix: bfloat16 [1024, 512], P(('grp', 'seq')), may hold values from -0.1875 to 0.1875
- output_weight: bfloat16 [1024, 1024], P(None, ('grp', 'seq')), may hold values from -0.75 to 0.75
- attention_gain: bfloat16 [1024], P(('grp', 'seq')), may hold values from 0.5 to 1.5
- expert_gain: bfloat16 [1024], P(('grp', 'seq')), may hold values from 0.5 to 1.5
- gate_up_weight: bfloat16 [32, 1024, 1024], P('seq', 'grp'), may hold values from -0.1875 to 0.1875
- down_weight: bfloat16 [32, 1024, 512], P('seq', 'grp'), may hold values from -0.25 to 0.25
Outputs:
- layer_output: bfloat16 [4096, 1024], P(('grp', 'seq'))
- input_grad: float32 [4096, 1024], P(('grp', 'seq'))
- query_grad: float32 [1024, 1024], P(('grp', 'seq'))
- key_grad: float32 [1024, 512], P(('grp', 'seq'))
- value_grad: float32 [1024, 512], P(('grp', 'seq'))
- output_grad: float32 [1024, 1024], P(None, ('grp', 'seq'))
- attention_gain_grad: float32 [1024], P(('grp', 'seq'))
- expert_gain_grad: float32 [1024], P(('grp', 'seq'))
- gate_up_grad: float32 [32, 1024, 1024], P('seq', 'grp')
- down_grad: float32 [32, 1024, 512], P('seq', 'grp')
The draws below stay inside these ranges and needn't reach their ends.
Inputs may be any that keep to these rules, and one draw needn't show every extreme that they name: `routes`: in the rows of one device no expert is named by more than 34 rows, a bound that some block reaches. `segments`: segment numbers never fall along the tokens; a segment holds at most 1024 tokens, and some segment exactly that many.
All inputs are finite; a program needn't handle non-finite values.
Results may differ from the reference program's by a relative error of at most 0.017.
Values may be sent and summed in bfloat16 or wider, within the bound.
No kernel may reach another device: no remote copies, remote signals or barrier semaphores. Data moves between devices by JAX's collectives and lax.ppermute only.
A program may use at most 192 MiB of HBM per device.

```python
import math
import jax
import jax.numpy as jnp
import numpy as np
from jax import lax

MODEL_DIMENSION = 1024
QUERY_HEADS = 16
KEY_VALUE_HEADS = 8
HEAD_SIZE = 64
E = 32
FF = 512
TOPK = 8
TOK_DEV = 128
CAP = 34
SEQUENCE_LENGTH = 1024
TOKEN_TOTAL = 4096


def steps_of(stream_key, dims, split, least, high):
    level = 1.0
    for axis_at, blocks in split:
        draws = jax.random.uniform(jax.random.fold_in(jax.random.fold_in(stream_key, 6), axis_at), (blocks,), jnp.float32, least / len(split), high / len(split))
        level = level * jnp.repeat(jnp.exp(draws), dims[axis_at] // blocks).reshape((-1,) + (1,) * (len(dims) - 1 - axis_at))
    return level


def split_up(number_of, total, limit, lean):
    loads = [(1 << 20) // math.isqrt(rank ** lean) + 1 for rank in range(2, number_of + 1)]
    rest, holding = total - limit - (number_of - 1), [1] * (number_of - 1)
    while rest > 0:
        free = [i for i in range(number_of - 1) if holding[i] < limit]
        whole, remaining = sum([loads[i] for i in free]), rest
        for i in free:
            extra = min(limit - holding[i], max(1, remaining * loads[i] // whole), rest)
            holding[i] = holding[i] + extra
            rest = rest - extra
    return np.array([limit] + holding)


def uneven(own_key, number_of, total, bound, slope):
    if number_of == 2:
        one = jax.random.randint(own_key, (), max(1, total - bound), min(bound, total - 1) + 1)
        return jnp.stack([one, total - one])
    tallies = jnp.asarray(split_up(number_of, total, bound, slope), jnp.int32)
    couples = (number_of - 1) // 2
    giver, sink = tallies[1:1 + 2 * couples:2], tallies[2:2 + 2 * couples:2]
    slack = jnp.minimum(giver - 1, bound - sink)
    shifted = jax.random.randint(jax.random.fold_in(own_key, 1), (couples,), 0, 1 << 20) % (slack + 1)
    tallies = tallies.at[1:1 + 2 * couples:2].set(giver - shifted).at[2:2 + 2 * couples:2].set(sink + shifted)
    return tallies[jax.random.permutation(jax.random.fold_in(own_key, 2), number_of)]


def routed_block(rng, own, number, rows, amount, top, reach, lean):
    order = jax.random.permutation(rng, amount)
    heavy_load, ordinary = shares(amount, rows * top, reach, lean, True), shares(amount, rows * top, reach, lean, False)
    places = jnp.arange(amount)

    def named(sizes, turn):
        used = int((sizes > 0).sum())
        fixed = max(1, used // 4)
        moved = fixed + (places - fixed + turn * (used - fixed)) % max(1, amount - fixed)
        return jnp.zeros((amount,), jnp.int32).at[order[jnp.where(places < fixed, places, moved)]].set(jnp.asarray(sizes, jnp.int32))

    sizes = jnp.where(number % 4 == 0, named(heavy_load, number // 4), named(ordinary, number - number // 4 - 1))
    mixed = jax.random.permutation(jax.random.fold_in(own, 3), amount)
    donor, receiver = mixed[0:amount // 2 * 2:2], mixed[1:amount // 2 * 2:2]
    room = jnp.minimum(sizes[donor] - 1, reach - sizes[receiver]) // 2
    room = jnp.where((donor == order[0]) | (receiver == order[0]) | (sizes[receiver] == 0), 0, jnp.maximum(room, 0))
    moved = jax.random.randint(jax.random.fold_in(own, 4), (amount // 2,), 0, 1 << 20) % (room + 1)
    sizes = sizes.at[donor].add(-moved).at[receiver].add(moved)
    items = jnp.searchsorted(jnp.cumsum(sizes), jnp.arange(rows * top), side="right").astype(jnp.int32)
    grid = items.reshape(top, rows).T
    grid = grid[jax.random.permutation(jax.random.fold_in(own, 1), rows)]
    turn = jax.random.randint(jax.random.fold_in(own, 2), (rows, 1), 0, top)
    return jnp.take_along_axis(grid, (jnp.arange(top)[None, :] + turn) % top, axis=1)


def shares(count, total, most, skew, full):
    loads = [(1 << 20) // math.isqrt(rank ** skew) + 1 for rank in range(1, count + 1)]
    largest = most if full else min(most, max(-(-total // count), total * loads[0] // sum(loads)))
    least = 1 if total - largest >= count - 1 else 0
    given, surplus = [largest] + [least] * (count - 1), total - largest - least * (count - 1)
    while surplus > 0:
        candidates = [i for i in range(1, count) if given[i] < largest] or [i for i in range(1, count) if given[i] < most]
        mass, budget = sum([loads[i] for i in candidates]), surplus
        for i in candidates:
            extra = min(most - given[i], max(1, budget * loads[i] // mass), surplus)
            given[i] = given[i] + extra
            surplus = surplus - extra
    return np.array(given)


def scatter_about(stream_key, shape, scale, limit, cuts=(), held_as=jnp.bfloat16):
    loudness = steps_of(stream_key, shape, cuts, -0.22, 0.18) if cuts else 1.0
    array = jax.random.normal(stream_key, shape, jnp.float32) * scale * loudness
    return jnp.minimum(jnp.maximum(array, -limit), limit).astype(held_as)


def setup_inputs(seed: int = 0) -> dict:
    streams_of = jax.random.split(jax.random.key(seed), 14)
    layer_input = scatter_about(streams_of[0], (TOKEN_TOTAL, MODEL_DIMENSION), 1.0, 6.0, ((0, 32),))
    segments = jnp.searchsorted(jnp.cumsum(uneven(streams_of[1], TOKEN_TOTAL // (SEQUENCE_LENGTH // 2), TOKEN_TOTAL, SEQUENCE_LENGTH, 1)), jnp.arange(TOKEN_TOTAL), side="right").astype(jnp.int32)
    routes_keys = jax.random.split(jax.random.fold_in(streams_of[2], 1), TOKEN_TOTAL // TOK_DEV)
    routes_turns = jax.random.permutation(jax.random.fold_in(streams_of[2], 3), TOKEN_TOTAL // TOK_DEV)
    routes = jax.vmap(lambda own, number: routed_block(jax.random.fold_in(streams_of[2], 2), own, number, TOK_DEV, E, TOPK, CAP, 1))(routes_keys, routes_turns).reshape((TOKEN_TOTAL, TOPK))
    gate_probs = jnp.clip(0.05 + 0.25 * jax.random.uniform(streams_of[3], (TOKEN_TOTAL, TOPK), jnp.float32) ** steps_of(streams_of[3], (TOKEN_TOTAL, TOPK), ((0, 32),), -0.2, 0.2), 0.05, 0.3)
    cotangent = scatter_about(streams_of[4], (TOKEN_TOTAL, MODEL_DIMENSION), 1.0, 6.0, ((0, 32),))
    query_weight = scatter_about(streams_of[5], (MODEL_DIMENSION, QUERY_HEADS * HEAD_SIZE), MODEL_DIMENSION ** -0.5, 0.1875, ((0, 32),))
    key_matrix = scatter_about(streams_of[6], (MODEL_DIMENSION, KEY_VALUE_HEADS * HEAD_SIZE), MODEL_DIMENSION ** -0.5, 0.1875, ((0, 32),))
    value_matrix = scatter_about(streams_of[7], (MODEL_DIMENSION, KEY_VALUE_HEADS * HEAD_SIZE), MODEL_DIMENSION ** -0.5, 0.1875, ((0, 32),))
    output_weight = scatter_about(streams_of[8], (QUERY_HEADS * HEAD_SIZE, MODEL_DIMENSION), (QUERY_HEADS * HEAD_SIZE // 16) ** -0.5, 0.75, ((1, 32),))
    attention_gain = jnp.clip(1.0 + 0.1 * jax.random.normal(streams_of[9], (MODEL_DIMENSION,), jnp.float32), 0.5, 1.5).astype(jnp.bfloat16)
    expert_gain = jnp.clip(1.0 + 0.1 * jax.random.normal(streams_of[10], (MODEL_DIMENSION,), jnp.float32), 0.5, 1.5).astype(jnp.bfloat16)
    gate_up_weight = scatter_about(streams_of[11], (E, MODEL_DIMENSION, 2 * FF), MODEL_DIMENSION ** -0.5, 0.1875, ((0, 8), (1, 4)))
    down_weight = scatter_about(streams_of[12], (E, MODEL_DIMENSION, FF), FF ** -0.5, 0.25, ((0, 8), (1, 4)))
    return dict(layer_input=layer_input, segments=segments, routes=routes, gate_probs=gate_probs, cotangent=cotangent, query_weight=query_weight, key_matrix=key_matrix, value_matrix=value_matrix, output_weight=output_weight, attention_gain=attention_gain, expert_gain=expert_gain, gate_up_weight=gate_up_weight, down_weight=down_weight)


EPS = 1e-06
THETA = 10000.0
NEGATIVE_LARGE = -1e+30

def rope_tables(position):
    half_dim = HEAD_SIZE // 2
    frequency = THETA ** (-2.0 * jnp.arange(half_dim, dtype=jnp.float32) / HEAD_SIZE)
    angles = position.astype(jnp.float32)[:, None] * frequency[None, :]
    return (jnp.cos(angles), jnp.sin(angles))

def rotate(vectors, cosine_table, sine_table):
    half_dim = vectors.shape[-1] // 2
    leading = vectors[..., :half_dim]
    trailing = vectors[..., half_dim:]
    cos_part = cosine_table[:, None, :]
    sin_part = sine_table[:, None, :]
    return jnp.concatenate([leading * cos_part - trailing * sin_part, trailing * cos_part + leading * sin_part], axis=-1)

def inverse_rotation(vectors, cosine_table, sine_table):
    half_dim = vectors.shape[-1] // 2
    leading = vectors[..., :half_dim]
    trailing = vectors[..., half_dim:]
    cos_part = cosine_table[:, None, :]
    sin_part = sine_table[:, None, :]
    return jnp.concatenate([leading * cos_part + trailing * sin_part, trailing * cos_part - leading * sin_part], axis=-1)

def norm_forward(inputs, gain_vector):
    floats = inputs.astype(jnp.float32)
    inverse = lax.rsqrt(lax.optimization_barrier(jnp.mean(floats * floats, axis=-1, keepdims=True)) + EPS)
    return (floats, inverse, (floats * inverse * gain_vector.astype(jnp.float32)).astype(jnp.bfloat16))

def norm_backward(floats, inverse, gain_vector, upstream):
    scaled = floats * inverse
    weighted = upstream * gain_vector.astype(jnp.float32)
    gain_part = lax.optimization_barrier(jnp.sum(upstream * scaled, axis=0))
    backward_part = inverse * (weighted - scaled * lax.optimization_barrier(jnp.mean(weighted * scaled, axis=-1, keepdims=True)))
    return (backward_part, gain_part)

def attend_sequence(packed):
    sequence_queries, sequence_keys, sequence_values, sequence_segments = packed
    sequence_extent = sequence_queries.shape[0]
    block_length = min(512, sequence_extent)
    score_scale = 1.0 / math.sqrt(HEAD_SIZE)
    key_position = jnp.arange(sequence_extent, dtype=jnp.int32)
    key_single_precision = sequence_keys.astype(jnp.float32)
    value_float = sequence_values.astype(jnp.float32)

    def one_block(block_index):
        offset = block_index * block_length
        query_block = lax.dynamic_slice_in_dim(sequence_queries, offset, block_length, 0).astype(jnp.float32)
        query_position = offset + jnp.arange(block_length, dtype=jnp.int32)
        query_segment = lax.dynamic_slice_in_dim(sequence_segments, offset, block_length, 0)
        scores = jnp.einsum('tgqd,ngd->tgqn', query_block, key_single_precision) * score_scale
        allowed = ((key_position[None, :] <= query_position[:, None]) & (sequence_segments[None, :] == query_segment[:, None]))[:, None, None, :]
        masked = jnp.where(allowed, scores, NEGATIVE_LARGE)
        row_max = lax.optimization_barrier(jnp.max(masked, axis=-1))
        weights = jnp.where(allowed, jnp.exp(masked - row_max[..., None]), 0.0)
        row_total = lax.optimization_barrier(jnp.sum(weights, axis=-1))
        weights_half = lax.optimization_barrier(weights.astype(jnp.bfloat16)).astype(jnp.float32)
        weighted_sum = jnp.einsum('tgqn,ngd->tgqd', weights_half, value_float)
        return ((weighted_sum / row_total[..., None]).astype(jnp.bfloat16), row_max + jnp.log(row_total))
    output_rows, log_sum_totals = lax.map(one_block, jnp.arange(sequence_extent // block_length, dtype=jnp.int32))
    head_group_ratio = QUERY_HEADS // KEY_VALUE_HEADS
    return (output_rows.reshape(sequence_extent, KEY_VALUE_HEADS, head_group_ratio, HEAD_SIZE), log_sum_totals.reshape(sequence_extent, KEY_VALUE_HEADS, head_group_ratio))

def attention_backward(packed):
    sequence_queries, sequence_keys, sequence_values, sequence_segments, seq_log_totals, seq_grads, seq_delta = packed
    sequence_extent = sequence_queries.shape[0]
    block_length = min(512, sequence_extent)
    score_scale = 1.0 / math.sqrt(HEAD_SIZE)
    key_position = jnp.arange(sequence_extent, dtype=jnp.int32)
    key_single_precision = sequence_keys.astype(jnp.float32)
    value_float = sequence_values.astype(jnp.float32)

    def one_block(totals, block_index):
        key_accumulator, value_accumulator = totals
        offset = block_index * block_length
        query_block = lax.dynamic_slice_in_dim(sequence_queries, offset, block_length, 0).astype(jnp.float32)
        grad_block = lax.dynamic_slice_in_dim(seq_grads, offset, block_length, 0).astype(jnp.float32)
        log_block = lax.dynamic_slice_in_dim(seq_log_totals, offset, block_length, 0)
        delta_block = lax.dynamic_slice_in_dim(seq_delta, offset, block_length, 0)
        query_position = offset + jnp.arange(block_length, dtype=jnp.int32)
        query_segment = lax.dynamic_slice_in_dim(sequence_segments, offset, block_length, 0)
        scores = jnp.einsum('tgqd,ngd->tgqn', query_block, key_single_precision) * score_scale
        allowed = ((key_position[None, :] <= query_position[:, None]) & (sequence_segments[None, :] == query_segment[:, None]))[:, None, None, :]
        probabilities = jnp.where(allowed, jnp.exp(jnp.where(allowed, scores, NEGATIVE_LARGE) - log_block[..., None]), 0.0)
        probs_half = lax.optimization_barrier(probabilities.astype(jnp.bfloat16)).astype(jnp.float32)
        value_accumulator = value_accumulator + jnp.einsum('tgqn,tgqd->ngd', probs_half, grad_block)
        prob_grad = jnp.einsum('tgqd,ngd->tgqn', grad_block, value_float)
        score_grad = lax.optimization_barrier((probabilities * (prob_grad - delta_block[..., None])).astype(jnp.bfloat16)).astype(jnp.float32)
        query_grad = jnp.einsum('tgqn,ngd->tgqd', score_grad, key_single_precision) * score_scale
        key_accumulator = key_accumulator + jnp.einsum('tgqn,tgqd->ngd', score_grad, query_block) * score_scale
        return ((key_accumulator, value_accumulator), query_grad)
    empty_key_value = jnp.zeros((sequence_extent, KEY_VALUE_HEADS, HEAD_SIZE), jnp.float32)
    (key_accumulator, value_accumulator), query_gradients = lax.scan(one_block, (empty_key_value, empty_key_value), jnp.arange(sequence_extent // block_length, dtype=jnp.int32))
    return (query_gradients.reshape(sequence_extent, KEY_VALUE_HEADS, QUERY_HEADS // KEY_VALUE_HEADS, HEAD_SIZE), key_accumulator, value_accumulator)

def reference(layer_input, segments, routes, gate_probs, cotangent, query_weight, key_matrix, value_matrix, output_weight, attention_gain, expert_gain, gate_up_weight, down_weight):
    head_group_ratio = QUERY_HEADS // KEY_VALUE_HEADS
    sequence_count = TOKEN_TOTAL // SEQUENCE_LENGTH
    position = jnp.arange(TOKEN_TOTAL, dtype=jnp.int32) % SEQUENCE_LENGTH
    cosine_table, sine_table = rope_tables(position)
    input_float, inverse_one, first_normed = norm_forward(layer_input, attention_gain)
    query_float = jnp.dot(first_normed, query_weight, preferred_element_type=jnp.float32).reshape(TOKEN_TOTAL, QUERY_HEADS, HEAD_SIZE)
    query_rows = rotate(query_float, cosine_table, sine_table).astype(jnp.bfloat16)
    key_single_precision = jnp.dot(first_normed, key_matrix, preferred_element_type=jnp.float32).reshape(TOKEN_TOTAL, KEY_VALUE_HEADS, HEAD_SIZE)
    key_rotated = rotate(key_single_precision, cosine_table, sine_table).astype(jnp.bfloat16)
    value_row_block = jnp.dot(first_normed, value_matrix, preferred_element_type=jnp.float32).astype(jnp.bfloat16).reshape(TOKEN_TOTAL, KEY_VALUE_HEADS, HEAD_SIZE)
    sequence_queries = query_rows.reshape(sequence_count, SEQUENCE_LENGTH, KEY_VALUE_HEADS, head_group_ratio, HEAD_SIZE)
    sequence_keys = key_rotated.reshape(sequence_count, SEQUENCE_LENGTH, KEY_VALUE_HEADS, HEAD_SIZE)
    sequence_values = value_row_block.reshape(sequence_count, SEQUENCE_LENGTH, KEY_VALUE_HEADS, HEAD_SIZE)
    sequence_segments = segments.reshape(sequence_count, SEQUENCE_LENGTH)
    attention_output, log_sum_totals = lax.map(attend_sequence, (sequence_queries, sequence_keys, sequence_values, sequence_segments))
    attention_output = attention_output.reshape(TOKEN_TOTAL, QUERY_HEADS * HEAD_SIZE)
    residual = input_float + jnp.dot(attention_output, output_weight, preferred_element_type=jnp.float32)
    residual, inverse_two, normed_two = norm_forward(residual, expert_gain)
    cot_float = cotangent.astype(jnp.float32)
    flat_experts = routes.reshape(-1).astype(jnp.int32)
    order = jnp.argsort(flat_experts, stable=True).astype(jnp.int32)
    counts = lax.optimization_barrier(jnp.sum((flat_experts[:, None] == jnp.arange(E, dtype=jnp.int32)[None, :]).astype(jnp.int32), axis=0)).astype(jnp.int32)
    offsets = (jnp.cumsum(counts) - counts).astype(jnp.int32)
    most_rows = CAP * (TOKEN_TOTAL // TOK_DEV)
    padded_order = jnp.concatenate([order, jnp.zeros((most_rows,), jnp.int32)])
    flat_probs = gate_probs.reshape(-1)

    def expert_step(totals, expert):
        mixture, normed_two_grad = totals
        picked = lax.dynamic_slice_in_dim(padded_order, offsets[expert], most_rows)
        live_rows = jnp.arange(most_rows, dtype=jnp.int32) < counts[expert]
        token_ids = (picked // TOPK).astype(jnp.int32)
        weight_rows = jnp.where(live_rows, flat_probs[picked], 0.0)
        rows_in = normed_two[token_ids] * live_rows[:, None].astype(jnp.bfloat16)
        upgate = jnp.dot(rows_in, gate_up_weight[expert], preferred_element_type=jnp.float32)
        gate_part = upgate[:, :FF]
        up_part = upgate[:, FF:]
        active = (jax.nn.silu(gate_part) * up_part).astype(jnp.bfloat16)
        produced = lax.optimization_barrier(jnp.dot(active, down_weight[expert].T, preferred_element_type=jnp.float32).astype(jnp.bfloat16))
        mixture = mixture.at[token_ids].add(weight_rows[:, None] * produced.astype(jnp.float32))
        route_cot = (weight_rows[:, None] * cot_float[token_ids]).astype(jnp.bfloat16)
        active_grad = jnp.dot(route_cot, down_weight[expert], preferred_element_type=jnp.float32)
        sigmoid_gate = jax.nn.sigmoid(gate_part)
        silu_gate = gate_part * sigmoid_gate
        upgate_grad = jnp.concatenate([active_grad * up_part * sigmoid_gate * (1.0 + gate_part * (1.0 - sigmoid_gate)), active_grad * silu_gate], axis=-1).astype(jnp.bfloat16)
        route_grad = lax.optimization_barrier(jnp.dot(upgate_grad, gate_up_weight[expert].T, preferred_element_type=jnp.float32).astype(jnp.bfloat16))
        normed_two_grad = normed_two_grad.at[token_ids].add(route_grad.astype(jnp.float32))
        down_part = jnp.dot(route_cot.T, active, preferred_element_type=jnp.float32)
        up_part_grad = jnp.dot(rows_in.T, upgate_grad, preferred_element_type=jnp.float32)
        return ((mixture, normed_two_grad), (up_part_grad, down_part))
    zero_rows = jnp.zeros((TOKEN_TOTAL, MODEL_DIMENSION), jnp.float32)
    (mixture, normed_two_grad), (gate_up_grad, down_grad) = lax.scan(expert_step, (zero_rows, zero_rows), jnp.arange(E, dtype=jnp.int32))
    layer_output = (residual + mixture).astype(jnp.bfloat16)
    residual_back, expert_gain_grad = norm_backward(residual, inverse_two, expert_gain, normed_two_grad)
    residual_grad = cot_float + residual_back
    residual_half = residual_grad.astype(jnp.bfloat16)
    output_grad = jnp.dot(attention_output.T, residual_half, preferred_element_type=jnp.float32)
    attention_output_grad = jnp.dot(residual_half, output_weight.T, preferred_element_type=jnp.float32).astype(jnp.bfloat16)
    grouped_gradient = attention_output_grad.reshape(TOKEN_TOTAL, KEY_VALUE_HEADS, head_group_ratio, HEAD_SIZE)
    delta_row_values = lax.optimization_barrier(jnp.sum(grouped_gradient.astype(jnp.float32) * attention_output.reshape(TOKEN_TOTAL, KEY_VALUE_HEADS, head_group_ratio, HEAD_SIZE).astype(jnp.float32), axis=-1))
    query_unrotated, key_unrotated, value_unprojected = lax.map(attention_backward, (sequence_queries, sequence_keys, sequence_values, sequence_segments, log_sum_totals, grouped_gradient.reshape(sequence_count, SEQUENCE_LENGTH, KEY_VALUE_HEADS, head_group_ratio, HEAD_SIZE), delta_row_values.reshape(sequence_count, SEQUENCE_LENGTH, KEY_VALUE_HEADS, head_group_ratio)))
    query_in = inverse_rotation(query_unrotated.reshape(TOKEN_TOTAL, QUERY_HEADS, HEAD_SIZE), cosine_table, sine_table).astype(jnp.bfloat16).reshape(TOKEN_TOTAL, QUERY_HEADS * HEAD_SIZE)
    key_input = inverse_rotation(key_unrotated.reshape(TOKEN_TOTAL, KEY_VALUE_HEADS, HEAD_SIZE), cosine_table, sine_table).astype(jnp.bfloat16).reshape(TOKEN_TOTAL, KEY_VALUE_HEADS * HEAD_SIZE)
    value_input = value_unprojected.reshape(TOKEN_TOTAL, KEY_VALUE_HEADS * HEAD_SIZE).astype(jnp.bfloat16)
    query_grad = jnp.dot(first_normed.T, query_in, preferred_element_type=jnp.float32)
    key_grad = jnp.dot(first_normed.T, key_input, preferred_element_type=jnp.float32)
    value_grad = jnp.dot(first_normed.T, value_input, preferred_element_type=jnp.float32)
    normed_one_grad = jnp.dot(query_in, query_weight.T, preferred_element_type=jnp.float32) + jnp.dot(key_input, key_matrix.T, preferred_element_type=jnp.float32) + jnp.dot(value_input, value_matrix.T, preferred_element_type=jnp.float32)
    input_back, attention_gain_grad = norm_backward(input_float, inverse_one, attention_gain, normed_one_grad)
    input_grad = residual_grad + input_back
    return (layer_output, input_grad, query_grad, key_grad, value_grad, output_grad, attention_gain_grad, expert_gain_grad, gate_up_grad, down_grad)
```

```python
import math

import jax
import jax.numpy as jnp
from jax import lax
from jax.sharding import PartitionSpec as P

QUERY_HEADS = 16
KEY_VALUE_HEADS = 8
HEAD_SIZE = 64
E = 32
CAP = 34
EPS = 1e-06
THETA = 10000.0
NEG = -1e30
BF = jnp.bfloat16
F32 = jnp.float32


def rope_full(length):
    half = HEAD_SIZE // 2
    frequency = THETA ** (-2.0 * jnp.arange(half, dtype=F32) / HEAD_SIZE)
    angles = jnp.arange(length, dtype=jnp.int32).astype(F32)[:, None] * frequency[None, :]
    return jnp.cos(angles), jnp.sin(angles)


def rotate(v, c, s):
    half = v.shape[-1] // 2
    a, b = v[..., :half], v[..., half:]
    c, s = c[:, None, :], s[:, None, :]
    return jnp.concatenate([a * c - b * s, b * c + a * s], axis=-1)


def dot(a, b, dims):
    return lax.dot_general(a, b, dims, preferred_element_type=F32)


NN = (((1,), (0,)), ((), ()))
NT = (((1,), (1,)), ((), ()))
TN = (((0,), (0,)), ((), ()))


class Ring:
    def __init__(self, n):
        self.n = n
        self.order = list(range(0, n, 2)) + list(range(n - 1, 0, -2))
        self.place = [self.order.index(i) for i in range(n)]

    def shift(self, a, k):
        n, o = self.n, self.order
        return lax.ppermute(a, "seq", [(o[i], o[(i + k) % n]) for i in range(n)])

    def gather(self, a):
        n = self.n
        half = n // 2
        r = {0: a}
        for j in range(1, half):
            r[j] = self.shift(r[j - 1], 1)
            r[n - j] = self.shift(r[(n - j + 1) % n], -1)
        h = a.shape[0] // 2
        r[half] = jnp.concatenate(
            [self.shift(r[half - 1][:h], 1), self.shift(r[half + 1][h:], -1)], axis=0
        )
        return [r[j] for j in range(n)]

    def scatter_sum(self, b):
        n = self.n
        half = n // 2
        h = b[0].shape[0] // 2

        def add(x, y):
            return (x.astype(F32) + y.astype(F32)).astype(BF)

        w = self.shift(b[half][:h], -1)
        f = self.shift(b[half][h:], 1)
        w = jnp.concatenate([add(w, b[half - 1][:h]), b[half - 1][h:]], axis=0)
        f = jnp.concatenate([b[half + 1][:h], add(f, b[half + 1][h:])], axis=0)
        for j in range(half - 2, 0, -1):
            w = add(self.shift(w, -1), b[j])
            f = add(self.shift(f, 1), b[n - j])
        w, f = self.shift(w, -1), self.shift(f, 1)
        return b[0].astype(F32) + w.astype(F32) + f.astype(F32)


def swap(a, bit, size):
    return lax.ppermute(a, "grp", [(i, i ^ bit) for i in range(size)])


def group_gather(a, size):
    pieces = {0: a}
    bit = size // 2
    while bit:
        for m in sorted(pieces):
            pieces[m | bit] = swap(pieces[m], bit, size)
        bit //= 2
    return [pieces[m] for m in range(size)]


def group_scatter_sum(pieces, size):
    pieces = dict(enumerate(pieces))
    bit = 1
    while bit < size:
        for m in sorted(pieces):
            if m & bit:
                other = swap(pieces.pop(m), bit, size)
                mine = pieces[m ^ bit]
                pieces[m ^ bit] = (mine.astype(F32) + other.astype(F32)).astype(BF)
        bit *= 2
    return pieces[0]


def body(
    layer_input,
    segments,
    routes,
    gate_probs,
    cotangent,
    query_weight,
    key_matrix,
    value_matrix,
    output_weight,
    attention_gain,
    expert_gain,
    gate_up_weight,
    down_weight,
):
    n = lax.axis_size("seq")
    groups = lax.axis_size("grp")
    tok, width = layer_input.shape
    length = n * tok
    local = gate_up_weight.shape[0]
    hidden = down_weight.shape[2]
    wrows = query_weight.shape[0]
    heads = QUERY_HEADS // n
    qw = heads * HEAD_SIZE
    pad = 2 * HEAD_SIZE - qw
    share = n // KEY_VALUE_HEADS
    scale = 1.0 / math.sqrt(HEAD_SIZE)
    slots = CAP * n
    ring = Ring(n)
    s = lax.axis_index("seq")
    g = lax.axis_index("grp")
    p = jnp.asarray(ring.place, jnp.int32)[s]
    source = jnp.asarray(ring.order, jnp.int32)[(p - jnp.arange(n)) % n]
    to_rel = (p - jnp.asarray(ring.place, jnp.int32)) % n
    xor_index = g ^ jnp.arange(groups)

    def absolute(blocks):
        return jnp.take(jnp.stack(blocks), to_rel, axis=0)

    wq = jnp.pad(query_weight.reshape(wrows, n, qw), ((0, 0), (0, 0), (0, pad)))
    wk = jnp.repeat(key_matrix.reshape(wrows, KEY_VALUE_HEADS, HEAD_SIZE), share, axis=1)
    wv = jnp.repeat(value_matrix.reshape(wrows, KEY_VALUE_HEADS, HEAD_SIZE), share, axis=1)
    wpack = jnp.concatenate([wq, wk, wv], axis=2)
    gains = jnp.stack([attention_gain, expert_gain], axis=1)
    extra = jnp.broadcast_to(jnp.pad(gains, ((0, 0), (0, 126)))[:, None, :], (wrows, n, 128))
    wsend = jnp.concatenate([wpack, extra], axis=2).transpose(1, 0, 2)
    wrecv = lax.all_to_all(wsend, "seq", split_axis=0, concat_axis=0, tiled=True)
    wpieces = group_gather(wrecv.reshape(n * wrows, 384), groups)
    whead = jnp.take(jnp.stack(wpieces), xor_index, axis=0).reshape(width, 384)
    gain_one = whead[:, 256].astype(F32)
    gain_two = whead[:, 257].astype(F32)
    whead = whead[:, :256]

    out_full = lax.all_gather(output_weight.T, ("grp", "seq"), axis=0, tiled=True)
    dense = jnp.sum(
        jnp.where(
            routes[:, :, None] == jnp.arange(E, dtype=jnp.int32), gate_probs[:, :, None], 0.0
        ),
        axis=1,
    )
    dense_hi = dense.astype(BF)
    dense_lo = (dense - dense_hi.astype(F32)).astype(BF)
    cot_block = jnp.concatenate(
        [cotangent, dense_hi, dense_lo, jnp.zeros((tok, 64), BF)], axis=1
    )
    cot_all = lax.all_gather(cot_block, "seq", axis=0, tiled=True)
    wfull = lax.all_gather(wpack.reshape(wrows, n * 256), ("grp", "seq"), axis=0, tiled=True)
    segment_block = jnp.broadcast_to(segments[:, None], (tok, 128))
    seg_all = absolute(ring.gather(segment_block))[:, :, 0].reshape(length)

    up_pieces = group_gather(gate_up_weight, groups)
    down_pieces = group_gather(down_weight, groups)

    x_all = absolute(ring.gather(layer_input)).reshape(length, width).astype(F32)
    inv_all = lax.rsqrt(jnp.mean(x_all * x_all, axis=-1, keepdims=True) + EPS)
    normed_all = (x_all * inv_all * gain_one).astype(BF)
    cos_t, sin_t = rope_full(length)
    qkv = dot(normed_all, whead, NN)
    q = rotate(qkv[:, :128].reshape(length, 2, HEAD_SIZE), cos_t, sin_t).astype(BF)
    k = rotate(qkv[:, 128:192].reshape(length, 1, HEAD_SIZE), cos_t, sin_t).astype(BF)[:, 0]
    v = qkv[:, 192:].astype(BF)
    pos = jnp.arange(length)
    allowed = ((pos[None, :] <= pos[:, None]) & (seg_all[None, :] == seg_all[:, None]))[None]
    scores = jnp.einsum("thd,nd->htn", q, k, preferred_element_type=F32) * scale
    scores = jnp.where(allowed, scores, NEG)
    top = jnp.max(scores, axis=-1)
    weights = jnp.where(allowed, jnp.exp(scores - top[..., None]), 0.0)
    total = jnp.sum(weights, axis=-1)
    lse = top + jnp.log(total)
    att = jnp.einsum("htn,nd->htd", weights.astype(BF), v, preferred_element_type=F32)
    att = (att / total[..., None]).astype(BF).transpose(1, 0, 2).reshape(length, 128)
    att_tok = lax.all_to_all(
        att.reshape(n, tok, 128), "seq", split_axis=0, concat_axis=0, tiled=True
    )
    att_tok = att_tok[:, :, :qw].transpose(1, 0, 2).reshape(tok, width)

    x_own = layer_input.astype(F32)
    residual = x_own + dot(att_tok, out_full, NT)
    inv_two = lax.rsqrt(jnp.mean(residual * residual, axis=-1, keepdims=True) + EPS)
    z_two = residual * inv_two
    n2_all = absolute(ring.gather((z_two * gain_two).astype(BF))).reshape(length, width)

    expert_up = jnp.take(jnp.stack(up_pieces), xor_index, axis=0).transpose(1, 0, 2, 3)
    expert_up = expert_up.reshape(local, width, 2 * hidden)
    expert_down = jnp.take(jnp.stack(down_pieces), xor_index, axis=0).transpose(1, 0, 2, 3)
    expert_down = expert_down.reshape(local, width, hidden)
    gates = cot_all[:, width : width + E].astype(F32) + cot_all[
        :, width + E : width + 2 * E
    ].astype(F32)
    gates = lax.dynamic_slice_in_dim(gates, s * local, local, axis=1).T
    cot_rows = cot_all[:, :width]
    mask = gates > 0
    rank = jnp.cumsum(mask.astype(jnp.int32), axis=1)
    slot = jnp.where(mask, rank - 1, -1)
    hit = slot[:, None, :] == jnp.arange(slots)[None, :, None]
    pick = hit.astype(BF)
    prob = jnp.sum(jnp.where(hit, gates[:, None, :], 0.0), axis=-1)[..., None]
    route_cot = (
        jnp.einsum("ect,td->ecd", pick, cot_rows, preferred_element_type=F32) * prob
    ).astype(BF)
    active_grad = jnp.einsum("ecd,edf->ecf", route_cot, expert_down, preferred_element_type=F32)
    rows_in = jnp.einsum("ect,td->ecd", pick, n2_all, preferred_element_type=F32).astype(BF)
    upgate = jnp.einsum("ecd,edf->ecf", rows_in, expert_up, preferred_element_type=F32)
    gate, up = upgate[..., :hidden], upgate[..., hidden:]
    sig = jax.nn.sigmoid(gate)
    silu = gate * sig
    active = (silu * up).astype(BF)
    upgate_grad = jnp.concatenate(
        [active_grad * up * sig * (1.0 + gate * (1.0 - sig)), active_grad * silu], axis=-1
    ).astype(BF)
    row_grads = jnp.einsum(
        "ecf,edf->ecd", upgate_grad, expert_up, preferred_element_type=F32
    ).astype(BF)
    n2g_part = jnp.einsum("ect,ecd->td", pick, row_grads, preferred_element_type=F32).astype(BF)
    n2g_part = jnp.take(n2g_part.reshape(n, tok, width), source, axis=0)
    n2g = ring.scatter_sum([n2g_part[r] for r in range(n)])

    produced = (
        jnp.einsum("ecf,edf->ecd", active, expert_down, preferred_element_type=F32) * prob
    ).astype(BF)
    mix_part = jnp.einsum("ect,ecd->td", pick, produced, preferred_element_type=F32).astype(BF)
    mixture = lax.psum_scatter(mix_part, "seq", scatter_dimension=0, tiled=True).astype(F32)
    layer_output = (residual + mixture).astype(BF)

    def shard_grad(a):
        cols = a.shape[-1]
        a = a.reshape(local, groups, width // groups, cols)
        a = jnp.take(a, xor_index, axis=1)
        return group_scatter_sum([a[:, m] for m in range(groups)], groups).astype(F32)

    gate_up_grad = shard_grad(
        jnp.einsum("ecd,ecf->edf", rows_in, upgate_grad, preferred_element_type=F32).astype(BF)
    )
    down_grad = shard_grad(
        jnp.einsum("ecd,ecf->edf", route_cot, active, preferred_element_type=F32).astype(BF)
    )

    cot_float = cotangent.astype(F32)
    g2 = n2g * gain_two
    residual_grad = cot_float + inv_two * (
        g2 - z_two * jnp.mean(g2 * z_two, axis=-1, keepdims=True)
    )
    gain_two_part = jnp.sum(n2g * z_two, axis=0)
    rh_all = absolute(ring.gather(residual_grad.astype(BF))).reshape(length, width)

    head_rows = lax.dynamic_slice_in_dim(out_full, s * qw, qw, axis=1)
    head_rows = jnp.pad(head_rows, ((0, 0), (0, pad)))
    att_grad = dot(rh_all, head_rows, NN).astype(BF)
    dwo = dot(rh_all, att, TN)
    do = att_grad.reshape(length, 2, HEAD_SIZE)
    delta = jnp.sum(
        do.astype(F32) * att.reshape(length, 2, HEAD_SIZE).astype(F32), axis=-1
    ).T
    probs = jnp.where(allowed, jnp.exp(scores - lse[..., None]), 0.0)
    dv = jnp.einsum("htn,thd->nd", probs.astype(BF), do, preferred_element_type=F32)
    dp = jnp.einsum("thd,nd->htn", do, v, preferred_element_type=F32)
    ds = (probs * (dp - delta[..., None])).astype(BF)
    dq = jnp.einsum("htn,nd->thd", ds, k, preferred_element_type=F32) * scale
    dk = jnp.einsum("htn,thd->nd", ds, q, preferred_element_type=F32) * scale
    dq = rotate(dq, cos_t, -sin_t).reshape(length, 128)
    dk = rotate(dk[:, None], cos_t, -sin_t).reshape(length, HEAD_SIZE)
    dqkv = jnp.concatenate([dq, dk, dv], axis=1).astype(BF)
    dqkv_tok = lax.all_to_all(
        dqkv.reshape(n, tok, 256), "seq", split_axis=0, concat_axis=0, tiled=True
    )
    dqkv_tok = dqkv_tok.transpose(1, 0, 2).reshape(tok, n * 256)
    dw = dot(normed_all, dqkv, TN)
    gain_hi = gain_two_part.astype(BF)
    gain_lo = (gain_two_part - gain_hi.astype(F32)).astype(BF)
    dw_all = jnp.concatenate(
        [
            dw.astype(BF),
            dwo.astype(BF),
            gain_hi[:, None],
            gain_lo[:, None],
            jnp.zeros((width, 126), BF),
        ],
        axis=1,
    )
    dw_all = jnp.take(dw_all.reshape(groups, width // groups, 512), xor_index, axis=0)
    dw_mine = group_scatter_sum([dw_all[m] for m in range(groups)], groups)
    dw_got = lax.all_to_all(
        dw_mine.reshape(n, wrows, 512), "seq", split_axis=0, concat_axis=0, tiled=True
    ).astype(F32)

    n1g = dot(dqkv_tok, wfull, NT)
    inv_one = lax.rsqrt(jnp.mean(x_own * x_own, axis=-1, keepdims=True) + EPS)
    z_one = x_own * inv_one
    g1 = n1g * gain_one
    input_grad = residual_grad + inv_one * (
        g1 - z_one * jnp.mean(g1 * z_one, axis=-1, keepdims=True)
    )

    query_grad = dw_got[:, :, :qw].transpose(1, 0, 2).reshape(wrows, -1)

    def pair_sum(a):
        a = a.reshape(KEY_VALUE_HEADS, share, wrows, HEAD_SIZE).sum(1)
        return a.transpose(1, 0, 2).reshape(wrows, -1)

    key_grad = pair_sum(dw_got[:, :, 128:192])
    value_grad = pair_sum(dw_got[:, :, 192:256])
    output_grad = dw_got[:, :, 256 : 256 + qw].transpose(0, 2, 1).reshape(-1, wrows)
    expert_gain_grad = jnp.sum(dw_got[:, :, 384] + dw_got[:, :, 385], axis=0)
    attention_gain_grad = (
        jnp.sum(query_grad * query_weight.astype(F32), axis=1)
        + jnp.sum(key_grad * key_matrix.astype(F32), axis=1)
        + jnp.sum(value_grad * value_matrix.astype(F32), axis=1)
    ) / attention_gain.astype(F32)
    return (
        layer_output,
        input_grad,
        query_grad,
        key_grad,
        value_grad,
        output_grad,
        attention_gain_grad,
        expert_gain_grad,
        gate_up_grad,
        down_grad,
    )


def solution(mesh):
    every = ("grp", "seq")
    rows = P(every, None)
    flat = P(every)
    expert = P("seq", "grp", None)
    columns = P(None, every)
    return jax.shard_map(
        body,
        mesh=mesh,
        in_specs=(
            rows, flat, rows, rows, rows, rows, rows, rows, columns, flat, flat, expert, expert,
        ),
        out_specs=(rows, rows, rows, rows, rows, columns, flat, flat, expert, expert),
        check_vma=False,
    )
```

```python
import math

import jax
import jax.numpy as jnp
from jax import lax
from jax.experimental import pallas as pl
from jax.experimental.pallas import tpu as pltpu
from jax.sharding import PartitionSpec as P

QUERY_HEADS = 16
KEY_VALUE_HEADS = 8
HEAD_SIZE = 64
E = 32
CAP = 34
EPS = 1e-06
THETA = 10000.0
NEG = -1e30
BF = jnp.bfloat16
F32 = jnp.float32


def rope_full(length):
    half = HEAD_SIZE // 2
    frequency = THETA ** (-2.0 * jnp.arange(half, dtype=F32) / HEAD_SIZE)
    angles = jnp.arange(length, dtype=jnp.int32).astype(F32)[:, None] * frequency[None, :]
    return jnp.cos(angles), jnp.sin(angles)


def rotate(v, c, s):
    half = v.shape[-1] // 2
    a, b = v[..., :half], v[..., half:]
    c, s = c[:, None, :], s[:, None, :]
    return jnp.concatenate([a * c - b * s, b * c + a * s], axis=-1)


def dot(a, b, dims):
    return lax.dot_general(a, b, dims, preferred_element_type=F32)


NN = (((1,), (0,)), ((), ()))
NT = (((1,), (1,)), ((), ()))
TN = (((0,), (0,)), ((), ()))


class Ring:
    def __init__(self, n):
        self.n = n
        self.order = list(range(0, n, 2)) + list(range(n - 1, 0, -2))
        self.place = [self.order.index(i) for i in range(n)]

    def shift(self, a, k):
        n, o = self.n, self.order
        return lax.ppermute(a, "seq", [(o[i], o[(i + k) % n]) for i in range(n)])

    def gather(self, a):
        n = self.n
        half = n // 2
        r = {0: a}
        for j in range(1, half):
            r[j] = self.shift(r[j - 1], 1)
            r[n - j] = self.shift(r[(n - j + 1) % n], -1)
        h = a.shape[0] // 2
        top = self.shift(r[half - 1][:h], 1)
        bottom = self.shift(r[half + 1][h:], -1)
        return [r[j] for j in range(n) if j != half] + [top, bottom]

    def scatter_sum(self, blocks):
        n = self.n
        half = n // 2
        top, bottom = blocks[n - 1], blocks[n]
        h = top.shape[0]
        b = {j: blocks[j - (j > half)] for j in range(n) if j != half}

        def add(x, y):
            return (x.astype(F32) + y.astype(F32)).astype(BF)

        w = self.shift(top, -1)
        f = self.shift(bottom, 1)
        w = jnp.concatenate([add(w, b[half - 1][:h]), b[half - 1][h:]], axis=0)
        f = jnp.concatenate([b[half + 1][:h], add(f, b[half + 1][h:])], axis=0)
        for j in range(half - 2, 0, -1):
            w = add(self.shift(w, -1), b[j])
            f = add(self.shift(f, 1), b[n - j])
        w, f = self.shift(w, -1), self.shift(f, 1)
        return b[0].astype(F32) + w.astype(F32) + f.astype(F32)


def swap(a, bit, size):
    return lax.ppermute(a, "grp", [(i, i ^ bit) for i in range(size)])


def group_gather(arrays, size, after):
    every = [{0: a} for a in arrays]
    bit = size // 2
    while bit:
        if bit == 1:
            flat = [q[m] for q in every for m in range(0, size, 2)]
            flat = iter(lax.optimization_barrier((after, *flat))[1:])
            every = [{m: next(flat) for m in range(0, size, 2)} for _ in every]
        for q in every:
            for m in sorted(q):
                q[m | bit] = swap(q[m], bit, size)
        bit //= 2
    return [[q[m] for m in range(size)] for q in every]


def simple_gather(a, size):
    pieces = {0: a}
    bit = size // 2
    while bit:
        for m in sorted(pieces):
            pieces[m | bit] = swap(pieces[m], bit, size)
        bit //= 2
    return [pieces[m] for m in range(size)]


def group_scatter_sum(pieces, size):
    pieces = dict(enumerate(pieces))
    bit = 1
    while bit < size:
        for m in sorted(pieces):
            if m & bit:
                other = swap(pieces.pop(m), bit, size)
                mine = pieces[m ^ bit]
                pieces[m ^ bit] = (mine.astype(F32) + other.astype(F32)).astype(BF)
        bit *= 2
    return pieces[0]


def iota(shape, axis):
    return lax.broadcasted_iota(jnp.int32, shape, axis)


def put_blocks(refs, scratch, index, n, tok):
    half = n // 2
    for i in range(n - 1):
        r = i + (i >= half)
        scratch[pl.ds(pl.multiple_of(index[r] * tok, tok), tok), :] = refs[i][...]
    h = tok // 2
    base = index[half] * tok
    scratch[pl.ds(pl.multiple_of(base, h), h), :] = refs[n - 1][...]
    scratch[pl.ds(pl.multiple_of(base + h, h), h), :] = refs[n][...]


def take_blocks(value, refs, index, n, tok):
    half = n // 2
    for i in range(n - 1):
        r = i + (i >= half)
        rows = pl.ds(pl.multiple_of(index[r] * tok, tok), tok)
        refs[i][...] = value[rows, :].astype(refs[i].dtype)
    h = tok // 2
    base = index[half] * tok
    refs[n - 1][...] = value[pl.ds(pl.multiple_of(base, h), h), :].astype(BF)
    refs[n][...] = value[pl.ds(pl.multiple_of(base + h, h), h), :].astype(BF)


def block_shapes(n, tok, width, dtype):
    return [jax.ShapeDtypeStruct((tok, width), dtype)] * (n - 1) + [
        jax.ShapeDtypeStruct((tok // 2, width), dtype)
    ] * 2


def put_pieces(refs, scratch, g):
    rows = refs[0].shape[1]
    for m in range(len(refs)):
        at = pl.multiple_of((g ^ m) * rows, rows)
        scratch[pl.ds(at, rows), :] = refs[m][0]


def take_pieces(value, refs, g):
    rows = refs[0].shape[1]
    for m in range(len(refs)):
        at = pl.multiple_of((g ^ m) * rows, rows)
        refs[m][0] = value[pl.ds(at, rows), :]


def whole(shape):
    return pl.BlockSpec(shape, lambda e, meta: (0,) * len(shape))


def per_expert(shape):
    return pl.BlockSpec((1,) + tuple(shape[1:]), lambda e, meta: (e, 0, 0))


def expert_call(body_fn, meta, ins, in_specs, outs, out_specs, scratch, flops, name):
    grid = next(a.shape[0] for a, q in zip(ins, in_specs) if q == "e")
    to_spec = lambda a, q: per_expert(a.shape) if q == "e" else whole(a.shape)
    bytes_moved = sum(math.prod(a.shape) * a.dtype.itemsize for a in list(ins) + list(outs))
    return pl.pallas_call(
        body_fn,
        out_shape=outs,
        grid_spec=pltpu.PrefetchScalarGridSpec(
            num_scalar_prefetch=1,
            grid=(grid,),
            in_specs=[to_spec(a, q) for a, q in zip(ins, in_specs)],
            out_specs=[to_spec(a, q) for a, q in zip(outs, out_specs)],
            scratch_shapes=scratch,
        ),
        compiler_params=pltpu.CompilerParams(
            dimension_semantics=("arbitrary",), vmem_limit_bytes=60 * 1024 * 1024
        ),
        cost_estimate=pl.CostEstimate(
            flops=flops, bytes_accessed=bytes_moved, transcendentals=0
        ),
        name=name,
    )(meta, *ins)


def sds(shape, dtype):
    return jax.ShapeDtypeStruct(shape, dtype)


def expert_prepare(meta, cot_all, down_pieces, n, tok, slots):
    groups = len(down_pieces)
    local, _, hidden = down_pieces[0].shape
    length = cot_all.shape[0]
    width = cot_all.shape[1] - 128

    def kernel(meta, cot, *refs):
        pieces = refs[:groups]
        rc_ref, ag_ref, prob_ref, slot_ref, slot_t_ref, dscr = refs[groups:]
        e = pl.program_id(0)
        lane = iota((tok, 128), 1)

        @pl.when(e == 0)
        def _():
            tri = (iota((tok, tok), 0) >= iota((tok, tok), 1)).astype(BF)
            seen = jnp.zeros((1, 128), F32)
            for b in range(n):
                gates = cot[b * tok : (b + 1) * tok, width:]
                mask = (gates.astype(F32) > 0) & (lane < E)
                ones = jnp.where(mask, 1.0, 0.0)
                rank = dot(tri, ones.astype(BF), NN) + seen
                seen = seen + jnp.sum(ones, axis=0, keepdims=True)
                slot = jnp.where(mask, rank - 1.0, -1.0)
                slot_ref[b * tok : (b + 1) * tok, :] = slot
                slot_t_ref[:, b * tok : (b + 1) * tok] = slot.T

        put_pieces(pieces, dscr, meta[1])
        expert = meta[0] * local + e
        row = slot_t_ref[pl.ds(expert, 1), :].astype(jnp.int32)
        pick = (iota((slots, length), 0) == row).astype(BF)
        got = dot(pick, cot[...], NN)
        lanes = iota((slots, 128), 1)
        chosen = (lanes == expert) | (lanes == expert + E)
        prob = jnp.sum(jnp.where(chosen, got[:, width:], 0.0), axis=1, keepdims=True)
        rc = (got[:, :width] * prob).astype(BF)
        rc_ref[0] = rc
        prob_ref[0] = jnp.broadcast_to(prob, (slots, 128))
        ag_ref[0] = dot(rc, dscr[...], NN)

    return expert_call(
        kernel,
        meta,
        [cot_all, *down_pieces],
        ["w"] + ["e"] * groups,
        [
            sds((local, slots, width), BF),
            sds((local, slots, hidden), F32),
            sds((local, slots, 128), F32),
            sds((length, 128), F32),
            sds((128, length), F32),
        ],
        ["e", "e", "e", "w", "w"],
        [pltpu.VMEM((width, hidden), BF)],
        local * 2 * slots * width * (length + hidden),
        "expert_prepare",
    )


def expert_rows(meta, n2_blocks, slot, slot_t, active_grad, up_pieces, n, tok):
    groups = len(up_pieces)
    local, _, double = up_pieces[0].shape
    hidden = double // 2
    slots = active_grad.shape[1]
    width = n2_blocks[0].shape[1]
    length = n * tok

    def kernel(meta, *refs):
        blocks = refs[: n + 1]
        slot_ref, slot_t_ref, ag_ref = refs[n + 1 : n + 4]
        pieces = refs[n + 4 : n + 4 + groups]
        outs = refs[n + 4 + groups :]
        rows_ref, ug_ref, act_ref = outs[:3]
        grads = outs[3 : n + 4]
        n2, wscr, acc = outs[n + 4 :]
        e = pl.program_id(0)

        @pl.when(e == 0)
        def _():
            put_blocks(blocks, n2, lambda_index(meta), n, tok)
            acc[...] = jnp.zeros_like(acc)

        put_pieces(pieces, wscr, meta[1])
        expert = meta[0] * local + e
        row = slot_t_ref[pl.ds(expert, 1), :].astype(jnp.int32)
        pick = (iota((slots, length), 0) == row).astype(BF)
        rows = dot(pick, n2[...], NN).astype(BF)
        rows_ref[0] = rows
        upgate = dot(rows, wscr[...], NN)
        gate, up = upgate[:, :hidden], upgate[:, hidden:]
        sig = jax.nn.sigmoid(gate)
        silu = gate * sig
        act_ref[0] = (silu * up).astype(BF)
        ag = ag_ref[0]
        ug_ref[0, :, :hidden] = (ag * up * sig * (1.0 + gate * (1.0 - sig))).astype(BF)
        ug_ref[0, :, hidden:] = (ag * silu).astype(BF)
        back = dot(ug_ref[0], wscr[...], NT).astype(BF)
        lane = iota((length, 128), 1)
        column = jnp.sum(jnp.where(lane == expert, slot_ref[...], 0.0), axis=1, keepdims=True)
        spread = (iota((length, slots), 1) == column.astype(jnp.int32)).astype(BF)
        acc[...] += dot(spread, back, NN)

        @pl.when(e == local - 1)
        def _():
            take_blocks(acc, grads, lambda_index(meta), n, tok)

    return expert_call(
        kernel,
        meta,
        [*n2_blocks, slot, slot_t, active_grad, *up_pieces],
        ["w"] * (n + 3) + ["e"] * (1 + groups),
        [
            sds((local, slots, width), BF),
            sds((local, slots, double), BF),
            sds((local, slots, hidden), BF),
            *block_shapes(n, tok, width, BF),
        ],
        ["e"] * 3 + ["w"] * (n + 1),
        [
            pltpu.VMEM((length, width), BF),
            pltpu.VMEM((width, double), BF),
            pltpu.VMEM((length, width), F32),
        ],
        local * 2 * slots * width * (2 * length + 2 * double),
        "expert_rows",
    )


class lambda_index:
    def __init__(self, meta):
        self.meta = meta

    def __getitem__(self, r):
        return self.meta[2 + r]


def expert_mix(meta, active, prob, slot, down_pieces):
    groups = len(down_pieces)
    local, slots, hidden = active.shape
    length = slot.shape[0]
    width = down_pieces[0].shape[1] * groups

    def kernel(meta, act_ref, prob_ref, slot_ref, *refs):
        pieces = refs[:groups]
        out, dscr, acc = refs[groups:]
        e = pl.program_id(0)
        put_pieces(pieces, dscr, meta[1])
        expert = meta[0] * local + e
        produced = (dot(act_ref[0], dscr[...], NT) * prob_ref[0][:, :1]).astype(BF)
        lane = iota((length, 128), 1)
        column = jnp.sum(jnp.where(lane == expert, slot_ref[...], 0.0), axis=1, keepdims=True)
        spread = (iota((length, slots), 1) == column.astype(jnp.int32)).astype(BF)
        add = dot(spread, produced, NN)

        @pl.when(e == 0)
        def _():
            acc[...] = add

        @pl.when(e > 0)
        def _():
            acc[...] += add

        @pl.when(e == local - 1)
        def _():
            out[...] = acc[...].astype(BF)

    return expert_call(
        kernel,
        meta,
        [active, prob, slot, *down_pieces],
        ["e", "e", "w"] + ["e"] * groups,
        [sds((length, width), BF)],
        ["w"],
        [pltpu.VMEM((width, hidden), BF), pltpu.VMEM((length, width), F32)],
        local * 2 * slots * width * (length + hidden),
        "expert_mix",
    )[0]


def expert_weights(meta, left, right, groups, name):
    local, slots, width = left.shape
    cols = right.shape[2]
    rows = width // groups

    def kernel(meta, a_ref, b_ref, *refs):
        outs, scr = refs[:groups], refs[groups]
        scr[...] = dot(a_ref[0], b_ref[0], TN).astype(BF)
        take_pieces(scr, outs, meta[1])

    return expert_call(
        kernel,
        meta,
        [left, right],
        ["e", "e"],
        [sds((local, rows, cols), BF)] * groups,
        ["e"] * groups,
        [pltpu.VMEM((width, cols), BF)],
        local * 2 * slots * width * cols,
        name,
    )


def single_call(kernel, meta, ins, outs, scratch, flops, name):
    bytes_moved = sum(math.prod(a.shape) * a.dtype.itemsize for a in list(ins) + list(outs))
    vmem = pl.BlockSpec(memory_space=pltpu.VMEM)
    return pl.pallas_call(
        kernel,
        out_shape=outs,
        in_specs=[pl.BlockSpec(memory_space=pltpu.SMEM)] + [vmem] * len(ins),
        out_specs=[vmem] * len(outs),
        scratch_shapes=scratch,
        compiler_params=pltpu.CompilerParams(vmem_limit_bytes=60 * 1024 * 1024),
        cost_estimate=pl.CostEstimate(
            flops=flops, bytes_accessed=bytes_moved, transcendentals=0
        ),
        name=name,
    )(meta, *ins)


def turn(v, cos_t, sin_t):
    lane = iota(v.shape, 1)
    other = jnp.where(
        lane % HEAD_SIZE < HEAD_SIZE // 2, pltpu.roll(v, 96, 1), pltpu.roll(v, 32, 1)
    )
    return v * cos_t + other * sin_t


def head_masks(rows):
    return iota((rows, 128), 1) < HEAD_SIZE


def attend(meta, x_blocks, whead, gain, cos_t, sin_t, seg_row, seg_col, n, tok):
    width = x_blocks[0].shape[1]
    length = n * tok
    bq = min(256, length)
    scale = 1.0 / math.sqrt(HEAD_SIZE)

    def kernel(meta, *refs):
        blocks = refs[: n + 1]
        w_ref, gain_ref, cos_ref, sin_ref, srow, scol = refs[n + 1 : n + 7]
        att_ref, q_ref, kv_ref, lse_ref, n1_ref = refs[n + 7 : n + 12]
        kdup, vdup = refs[n + 12 :]
        put_blocks(blocks, n1_ref, lambda_index(meta), n, tok)
        for b in range(n):
            rows = slice(b * tok, (b + 1) * tok)
            x = n1_ref[rows, :].astype(F32)
            inv = lax.rsqrt(jnp.mean(x * x, axis=-1, keepdims=True) + EPS)
            n1_ref[rows, :] = (x * inv * gain_ref[...]).astype(BF)
        qkv = dot(n1_ref[...], w_ref[...], NN)
        low = head_masks(length)
        cos_v, sin_v = cos_ref[...], sin_ref[...]
        q_ref[...] = (turn(qkv[:, :128], cos_v, sin_v) * scale).astype(BF)
        kv = qkv[:, 128:]
        kv = jnp.where(low, turn(kv, cos_v, sin_v), kv)
        kv_ref[...] = kv.astype(BF)
        swapped = pltpu.roll(kv, HEAD_SIZE, 1)
        kdup[...] = jnp.where(low, kv, swapped).astype(BF)
        vdup[...] = jnp.where(low, swapped, kv).astype(BF)
        low = head_masks(bq)
        for i in range(length // bq):
            rows = slice(i * bq, (i + 1) * bq)
            ext = (i + 1) * bq
            allowed = (iota((bq, ext), 1) <= iota((bq, ext), 0) + i * bq) & (
                srow[:, :ext] == scol[rows, :]
            )
            q = q_ref[rows, :]
            parts = []
            for h in range(2):
                qh = jnp.where(low == (h == 0), q, jnp.zeros_like(q))
                sc = jnp.where(allowed, dot(qh, kdup[:ext, :], NT), NEG)
                top = jnp.max(sc, axis=-1, keepdims=True)
                wts = jnp.exp(sc - top)
                total = jnp.sum(wts, axis=-1, keepdims=True)
                o = dot(wts.astype(BF), vdup[:ext, :], NN) / total
                parts.append((o, top + jnp.log(total)))
            att_ref[rows, :] = jnp.where(low, parts[0][0], parts[1][0]).astype(BF)
            lse_ref[rows, :] = jnp.where(low, parts[0][1], parts[1][1])

    return single_call(
        kernel,
        meta,
        [*x_blocks, whead, gain, cos_t, sin_t, seg_row, seg_col],
        [
            sds((length, 128), BF),
            sds((length, 128), BF),
            sds((length, 128), BF),
            sds((length, 128), F32),
            sds((length, width), BF),
        ],
        [pltpu.VMEM((length, 128), BF), pltpu.VMEM((length, 128), BF)],
        2 * length * width * 256 + 8 * length * length * 128,
        "attend",
    )


def attend_back(
    meta, rh_blocks, head_rows, att, q, kv, lse, n1, cos_t, sin_t, seg_row, seg_col, extra,
    n, tok, groups,
):
    width = n1.shape[1]
    length = n * tok
    bq = min(256, length)
    scale = 1.0 / math.sqrt(HEAD_SIZE)
    rows_g = width // groups

    def kernel(meta, *refs):
        blocks = refs[: n + 1]
        (wo, att_ref, q_ref, kv_ref, lse_ref, n1_ref, cos_ref, sin_ref, srow, scol, extra_ref) = (
            refs[n + 1 : n + 12]
        )
        dqkv_ref = refs[n + 12]
        pieces = refs[n + 13 : n + 13 + groups]
        rh, kdup, vdup, do_ref, dk, dv, dw = refs[n + 13 + groups :]
        put_blocks(blocks, rh, lambda_index(meta), n, tok)
        do_ref[...] = dot(rh[...], wo[...], NN).astype(BF)
        dw[:, 256:384] = dot(rh[...], att_ref[...], TN).astype(BF)
        dw[:, 384:] = extra_ref[...]
        low = head_masks(length)
        kv = kv_ref[...].astype(F32)
        swapped = pltpu.roll(kv, HEAD_SIZE, 1)
        kdup[...] = jnp.where(low, kv, swapped).astype(BF)
        vdup[...] = jnp.where(low, swapped, kv).astype(BF)
        dk[...] = jnp.zeros_like(dk)
        dv[...] = jnp.zeros_like(dv)
        low = head_masks(bq)
        for i in range(length // bq):
            rows = slice(i * bq, (i + 1) * bq)
            ext = (i + 1) * bq
            allowed = (iota((bq, ext), 1) <= iota((bq, ext), 0) + i * bq) & (
                srow[:, :ext] == scol[rows, :]
            )
            q = q_ref[rows, :]
            do = do_ref[rows, :]
            prod = do.astype(F32) * att_ref[rows, :].astype(F32)
            parts = []
            for h in range(2):
                mine = low == (h == 0)
                qh = jnp.where(mine, q, jnp.zeros_like(q))
                doh = jnp.where(mine, do, jnp.zeros_like(do))
                delta = jnp.sum(jnp.where(mine, prod, 0.0), axis=-1, keepdims=True)
                sc = dot(qh, kdup[:ext, :], NT)
                at = lse_ref[rows, h * HEAD_SIZE : h * HEAD_SIZE + 1]
                pr = jnp.exp(jnp.where(allowed, sc - at, NEG))
                dp = dot(doh, vdup[:ext, :], NT)
                ds = (pr * (dp - delta)).astype(BF)
                dv[:ext, :] += dot(pr.astype(BF), doh, TN)
                dk[:ext, :] += dot(ds, qh, TN)
                parts.append(dot(ds, kdup[:ext, :], NN))
            dq = jnp.where(low, parts[0], parts[1]) * scale
            dqkv_ref[rows, :128] = turn(dq, cos_ref[rows, :], -sin_ref[rows, :]).astype(BF)
        low = head_masks(length)
        dks = dk[...] + pltpu.roll(dk[...], HEAD_SIZE, 1)
        dvs = dv[...] + pltpu.roll(dv[...], HEAD_SIZE, 1)
        dks = turn(dks, cos_ref[...], -sin_ref[...])
        dqkv_ref[:, 128:] = jnp.where(low, dks, dvs).astype(BF)
        dw[:, :256] = dot(n1_ref[...], dqkv_ref[...], TN).astype(BF)
        g = meta[1]
        for m in range(groups):
            at = pl.multiple_of((g ^ m) * rows_g, rows_g)
            pieces[m][...] = dw[pl.ds(at, rows_g), :]

    return single_call(
        kernel,
        meta,
        [*rh_blocks, head_rows, att, q, kv, lse, n1, cos_t, sin_t, seg_row, seg_col, extra],
        [sds((length, 256), BF)] + [sds((rows_g, 512), BF)] * groups,
        [
            pltpu.VMEM((length, width), BF),
            pltpu.VMEM((length, 128), BF),
            pltpu.VMEM((length, 128), BF),
            pltpu.VMEM((length, 128), BF),
            pltpu.VMEM((length, 128), F32),
            pltpu.VMEM((length, 128), F32),
            pltpu.VMEM((width, 512), BF),
        ],
        2 * length * width * 512 + 20 * length * length * 128,
        "attend_back",
    )


def body(
    layer_input,
    segments,
    routes,
    gate_probs,
    cotangent,
    query_weight,
    key_matrix,
    value_matrix,
    output_weight,
    attention_gain,
    expert_gain,
    gate_up_weight,
    down_weight,
):
    n = lax.axis_size("seq")
    groups = lax.axis_size("grp")
    tok, width = layer_input.shape
    length = n * tok
    local = gate_up_weight.shape[0]
    hidden = down_weight.shape[2]
    wrows = query_weight.shape[0]
    heads = QUERY_HEADS // n
    qw = heads * HEAD_SIZE
    pad = 2 * HEAD_SIZE - qw
    share = n // KEY_VALUE_HEADS
    scale = 1.0 / math.sqrt(HEAD_SIZE)
    slots = CAP * n
    ring = Ring(n)
    s = lax.axis_index("seq")
    g = lax.axis_index("grp")
    p = jnp.asarray(ring.place, jnp.int32)[s]
    source = jnp.asarray(ring.order, jnp.int32)[(p - jnp.arange(n)) % n]
    xor_index = g ^ jnp.arange(groups)

    meta = jnp.concatenate([jnp.stack([s, g]).astype(jnp.int32), source.astype(jnp.int32)])

    wq = jnp.pad(query_weight.reshape(wrows, n, qw), ((0, 0), (0, 0), (0, pad)))
    wk = jnp.repeat(key_matrix.reshape(wrows, KEY_VALUE_HEADS, HEAD_SIZE), share, axis=1)
    wv = jnp.repeat(value_matrix.reshape(wrows, KEY_VALUE_HEADS, HEAD_SIZE), share, axis=1)
    wpack = jnp.concatenate([wq, wk, wv], axis=2)
    per_row = tok // wrows
    small = jnp.concatenate(
        [
            jnp.stack([attention_gain, expert_gain], axis=1),
            segments.reshape(wrows, per_row).astype(BF),
            jnp.zeros((wrows, 126 - per_row), BF),
        ],
        axis=1,
    )
    extra = jnp.broadcast_to(small[:, None, :], (wrows, n, 128))
    wsend = jnp.concatenate([wpack, extra], axis=2).transpose(1, 0, 2)
    wrecv = lax.all_to_all(wsend, "seq", split_axis=0, concat_axis=0, tiled=True)
    seg_row = wrecv[:, :, 258 : 258 + per_row].astype(jnp.int32).reshape(1, length)
    seg_col = seg_row.reshape(length, 1)
    wpieces = simple_gather(wrecv.reshape(n * wrows, 384), groups)
    whead = jnp.take(jnp.stack(wpieces), xor_index, axis=0).reshape(width, 384)
    gain_one = whead[:, 256].astype(F32)
    gain_two = whead[:, 257].astype(F32)
    whead = whead[:, :256]

    out_full = lax.all_gather(output_weight.T, ("grp", "seq"), axis=0, tiled=True)
    dense = jnp.sum(
        jnp.where(
            routes[:, :, None] == jnp.arange(E, dtype=jnp.int32), gate_probs[:, :, None], 0.0
        ),
        axis=1,
    )
    dense_hi = dense.astype(BF)
    dense_lo = (dense - dense_hi.astype(F32)).astype(BF)
    cot_block = jnp.concatenate(
        [cotangent, dense_hi, dense_lo, jnp.zeros((tok, 64), BF)], axis=1
    )
    cot_all = lax.all_gather(cot_block, "seq", axis=0, tiled=True)
    wfull = lax.all_gather(wpack.reshape(wrows, n * 256), ("grp", "seq"), axis=0, tiled=True)

    cos_t, sin_t = rope_full(length)
    cos_t = jnp.concatenate([cos_t] * 4, axis=1)
    sin_t = jnp.concatenate([-sin_t, sin_t] * 2, axis=1)
    att, q, kv, lse, normed_all = attend(
        meta, ring.gather(layer_input), whead, gain_one[None, :], cos_t, sin_t, seg_row, seg_col,
        n, tok,
    )
    att_tok = lax.all_to_all(
        att.reshape(n, tok, 128), "seq", split_axis=0, concat_axis=0, tiled=True
    )
    down_pieces, up_pieces = group_gather([down_weight, gate_up_weight], groups, att_tok)
    att_tok = att_tok[:, :, :qw].transpose(1, 0, 2).reshape(tok, width)

    x_own = layer_input.astype(F32)
    residual = x_own + dot(att_tok, out_full, NT)
    inv_two = lax.rsqrt(jnp.mean(residual * residual, axis=-1, keepdims=True) + EPS)
    z_two = residual * inv_two
    n2_blocks = ring.gather((z_two * gain_two).astype(BF))

    route_cot, active_grad, prob, slot, slot_t = expert_prepare(
        meta, cot_all, down_pieces, n, tok, slots
    )
    outs = expert_rows(meta, n2_blocks, slot, slot_t, active_grad, up_pieces, n, tok)
    rows_in, upgate_grad, active = outs[:3]
    n2g = ring.scatter_sum(outs[3:])
    mix_part = expert_mix(meta, active, prob, slot, down_pieces)
    mixture = lax.psum_scatter(mix_part, "seq", scatter_dimension=0, tiled=True).astype(F32)
    layer_output = (residual + mixture).astype(BF)

    gate_up_grad = group_scatter_sum(
        expert_weights(meta, rows_in, upgate_grad, groups, "expert_up_grad"), groups
    ).astype(F32)
    down_grad = group_scatter_sum(
        expert_weights(meta, route_cot, active, groups, "expert_down_grad"), groups
    ).astype(F32)

    cot_float = cotangent.astype(F32)
    g2 = n2g * gain_two
    residual_grad = cot_float + inv_two * (
        g2 - z_two * jnp.mean(g2 * z_two, axis=-1, keepdims=True)
    )
    gain_two_part = jnp.sum(n2g * z_two, axis=0)
    rh_blocks = ring.gather(residual_grad.astype(BF))

    head_rows = lax.dynamic_slice_in_dim(out_full, s * qw, qw, axis=1)
    head_rows = jnp.pad(head_rows, ((0, 0), (0, pad)))
    gain_hi = gain_two_part.astype(BF)
    gain_lo = (gain_two_part - gain_hi.astype(F32)).astype(BF)
    extra = jnp.pad(jnp.stack([gain_hi, gain_lo], axis=1), ((0, 0), (0, 126)))
    dqkv, *dw_pieces = attend_back(
        meta, rh_blocks, head_rows, att, q, kv, lse, normed_all, cos_t, sin_t, seg_row, seg_col,
        extra, n, tok, groups,
    )
    dqkv_tok = lax.all_to_all(
        dqkv.reshape(n, tok, 256), "seq", split_axis=0, concat_axis=0, tiled=True
    )
    dqkv_tok = dqkv_tok.transpose(1, 0, 2).reshape(tok, n * 256)
    dw_mine = group_scatter_sum(dw_pieces, groups)
    dw_got = lax.all_to_all(
        dw_mine.reshape(n, wrows, 512), "seq", split_axis=0, concat_axis=0, tiled=True
    ).astype(F32)

    n1g = dot(dqkv_tok, wfull, NT)
    inv_one = lax.rsqrt(jnp.mean(x_own * x_own, axis=-1, keepdims=True) + EPS)
    z_one = x_own * inv_one
    g1 = n1g * gain_one
    input_grad = residual_grad + inv_one * (
        g1 - z_one * jnp.mean(g1 * z_one, axis=-1, keepdims=True)
    )

    query_grad = dw_got[:, :, :qw].transpose(1, 0, 2).reshape(wrows, -1)

    def pair_sum(a):
        a = a.reshape(KEY_VALUE_HEADS, share, wrows, HEAD_SIZE).sum(1)
        return a.transpose(1, 0, 2).reshape(wrows, -1)

    key_grad = pair_sum(dw_got[:, :, 128:192])
    value_grad = pair_sum(dw_got[:, :, 192:256])
    output_grad = dw_got[:, :, 256 : 256 + qw].transpose(0, 2, 1).reshape(-1, wrows)
    expert_gain_grad = jnp.sum(dw_got[:, :, 384] + dw_got[:, :, 385], axis=0)
    attention_gain_grad = (
        jnp.sum(query_grad * query_weight.astype(F32), axis=1)
        + jnp.sum(key_grad * key_matrix.astype(F32), axis=1)
        + jnp.sum(value_grad * value_matrix.astype(F32), axis=1)
    ) / attention_gain.astype(F32)
    return (
        layer_output,
        input_grad,
        query_grad,
        key_grad,
        value_grad,
        output_grad,
        attention_gain_grad,
        expert_gain_grad,
        gate_up_grad,
        down_grad,
    )


def solution(mesh):
    every = ("grp", "seq")
    rows = P(every, None)
    flat = P(every)
    expert = P("seq", "grp", None)
    columns = P(None, every)
    return jax.shard_map(
        body,
        mesh=mesh,
        in_specs=(
            rows, flat, rows, rows, rows, rows, rows, rows, columns, flat, flat, expert, expert,
        ),
        out_specs=(rows, rows, rows, rows, rows, columns, flat, flat, expert, expert),
        check_vma=False,
    )
```
